256 devices in a mesh: gx: 8 (over y, core), gy: 4 (over z_lo), gz: 8 (over z_hi, x).
Axes of the slice: x: 4, y: 4, z: 8 (z_hi: 2, z_lo: 4; z = z_hi * 4 + z_lo), core: 2. Of those that a mesh axis runs over, the one named last changes fastest.
Arguments:
- tokens: bfloat16 [2048, 8192], P(('gx', 'gy'), 'gz'), may hold values from -6 to 6
- gate_weight: bfloat16 [8192, 28672], P('gz', ('gx', 'gy')), may hold values from -0.0625 to 0.0625
- up_weight: bfloat16 [8192, 28672], P('gz', ('gx', 'gy')), may hold values from -0.0625 to 0.0625
- down_weight: bfloat16 [28672, 8192], P(('gx', 'gy'), 'gz'), may hold values from -0.03125 to 0.03125
Outputs:
- layer_output: bfloat16 [2048, 8192], P(('gx', 'gy'), 'gz')
The draws below stay inside these ranges and needn't reach their ends.
All inputs are finite; a program needn't handle non-finite values.
Results may differ from the reference program's by a relative error of at most 0.029.
Values may be sent and summed in bfloat16 or wider, within the bound.
A program may use at most 128 MiB of HBM per device.

```python
import jax
import jax.numpy as jnp
from jax import lax

D = 8192
FF = 28672
TOKENS = 2048
N_GZ = 8


def steps_of(rng, extent, split, least, high):
    level = 1.0
    for dim, shards_of in split:
        heights = jax.random.uniform(jax.random.fold_in(jax.random.fold_in(rng, 6), dim), (shards_of,), jnp.float32, least / len(split), high / len(split))
        level = level * jnp.repeat(jnp.exp(heights), extent[dim] // shards_of).reshape((-1,) + (1,) * (len(extent) - 1 - dim))
    return level


def noise(own_key, shape, scale, most, shards=(), dtype=jnp.bfloat16):
    factor_of = steps_of(own_key, shape, shards, -0.22, 0.18) if shards else 1.0
    result = jax.random.normal(own_key, shape, jnp.float32) * scale * factor_of
    return jnp.minimum(jnp.maximum(result, -most), most).astype(dtype)


def setup_inputs(seed: int = 0) -> dict:
    seeds = jax.random.split(jax.random.key(seed), 5)
    tokens = noise(seeds[0], (TOKENS, D), 1.0, 6.0, ((0, 32), (1, 8)))
    gate_weight = noise(seeds[1], (D, FF), D ** -0.5, 0.0625, ((0, 8), (1, 32)))
    up_weight = noise(seeds[2], (D, FF), D ** -0.5, 0.0625, ((0, 8), (1, 32)))
    down_weight = noise(seeds[3], (FF, D), FF ** -0.5, 0.03125, ((0, 32), (1, 8)))
    return dict(tokens=tokens, gate_weight=gate_weight, up_weight=up_weight, down_weight=down_weight)


def blocked_sum(tokens, weight_matrix):
    span_width = D // N_GZ
    running = jnp.zeros((tokens.shape[0], weight_matrix.shape[1]), jnp.float32)
    for segment in range(N_GZ):
        left_part = tokens[:, segment * span_width:(segment + 1) * span_width]
        right_part = weight_matrix[segment * span_width:(segment + 1) * span_width, :]
        product = jnp.dot(left_part, right_part, preferred_element_type=jnp.float32)
        rounded = lax.optimization_barrier(product.astype(jnp.bfloat16))
        running = running + rounded.astype(jnp.float32)
    return running


def reference(tokens, gate_weight, up_weight, down_weight):
    gate = blocked_sum(tokens, gate_weight)
    up_sum = blocked_sum(tokens, up_weight)
    hidden = (jax.nn.silu(gate) * up_sum).astype(jnp.bfloat16)
    return jnp.dot(hidden, down_weight, preferred_element_type=jnp.float32).astype(jnp.bfloat16)
```

```python
import functools

import jax
import jax.numpy as jnp
from jax import lax
from jax.experimental import pallas as pl
from jax.experimental.pallas import tpu as pltpu
from jax.sharding import PartitionSpec as P

PANELS = 4
BF16, F32 = jnp.bfloat16, jnp.float32
STEPS = ("A1", "A2", "A3", "A4", "M1", "X2", "Z1", "H", "E2", "E3", "M2", "G2", "G3", "G4", "G5")
COPIES = (
    "az1", "az2", "az3", "ayr", "ayl", "arr", "arl", "ac",
    "s1g", "s1u", "sug", "sgu", "lg", "lu", "z",
    "ez", "eor", "eol", "epr", "epl", "err", "erl",
    "gc", "y1a", "y1b", "ysb", "ysa", "yla", "ylb", "gz1", "gz2", "gz3",
)
SEM = {name: i for i, name in enumerate(COPIES)}


def step_order(panels):
    f = 4.0 / panels
    lat = 1.5
    table = dict(
        A1=((), 0.1, (("az", "z", 2.3),)),
        A2=(("az",), 0.1, (("ay", "y", 2.9),)),
        A3=(("ay",), 0.1, (("ar", "y", 1.5),)),
        A4=(("ar",), 0.1, (("ac", "c", 1.0),)),
        M1=(("ac",), 2.5, (("s1", "x", 5.0), ("sh", "x", 5.0))),
        X2=(("s1",), 0.5, (("lo", "x", 5.0),)),
        Z1=(("lo", "sh"), 1.0, (("zz", "z", 10.0),)),
        H=(("zz",), 1.0, (("ez", "z", 5.0), ("eo", "x", 2.5))),
        E2=(("ez",), 0.1, (("ep", "x", 2.5),)),
        E3=(("eo", "ep"), 0.1, (("er", "x", 2.5),)),
        M2=(("er",), 1.5, (("gc", "c", 1.0),)),
        G2=(("gc",), 1.0, (("y1", "y", 1.4), ("ys", "y", 1.4))),
        G3=(("y1",), 0.3, (("yl", "y", 1.4),)),
        G4=(("yl", "ys"), 0.5, (("gz", "z", 2.5),)),
        G5=(("gz",), 0.3, ()),
    )
    done, arrive, free = {}, {}, dict(x=0.0, y=0.0, z=0.0, c=0.0)
    now, order = 0.0, []
    while len(order) < panels * len(STEPS):
        best = None
        for p in range(panels):
            for i, s in enumerate(STEPS):
                if (p, s) in done:
                    continue
                if i and (p, STEPS[i - 1]) not in done:
                    break
                if p and (p - 1, s) not in done:
                    break
                if p and s == "M1" and (p - 1, "X2") not in done:
                    break
                ready = max([arrive[(p, m)] for m in table[s][0]] + [0.0])
                key = (max(ready, now), -i)
                if best is None or key < best[0]:
                    best = (key, p, s)
                break
        (start, _), p, s = best
        now = start + table[s][1] * f
        for name, link, time in table[s][2]:
            free[link] = max(free[link], now) + time * f
            arrive[(p, name)] = free[link] + lat
        done[(p, s)] = now
        order.append((p, s))
    return tuple(order)


def kernel(
    panels, tokens, gate_hbm, up_hbm, down_hbm, out,
    wgu, wd, tok, part, s1g, s1u, lg, sgu, lu, sug, zsend, zkeep, zrecv, hid, outp,
    crecv, osum, y1a, y1b, yla, ysa, ylb, ysb, zos, zor, send_sem, recv_sem, weight_sem,
):
    gx, gy, gz = lax.axis_index("gx"), lax.axis_index("gy"), lax.axis_index("gz")
    x, h, y, c, zl = lax.rem(gz, 4), gz // 4, gx // 2, lax.rem(gx, 2), gy
    r = 64 // panels
    rows = 4 * r
    half = rows // 2
    ff = gate_hbm.shape[1]
    mid = out.shape[1] // 2

    def mod4(v):
        return lax.rem(v + 4, 4)

    def device(x=x, h=h, y=y, c=c, zl=zl):
        return {"gx": 2 * y + c, "gy": zl, "gz": 4 * h + x}

    xr, xl = device(x=mod4(x + 1)), device(x=mod4(x - 1))
    yr, yl = device(y=mod4(y + 1)), device(y=mod4(y - 1))
    zpeer = device(h=1 - h)
    core = device(c=1 - c)
    zs = [None] + [device(zl=mod4(zl + k)) for k in (1, 2, 3)]

    barrier = pltpu.get_barrier_semaphore()
    peers = (xr, xl, yr, yl, zpeer, core, zs[1], zs[2], zs[3])
    for peer in peers:
        pl.semaphore_signal(barrier, inc=1, device_id=peer, device_id_type=pl.DeviceIdType.MESH)
    loads = [
        pltpu.make_async_copy(gate_hbm, wgu.at[:, pl.ds(0, ff)], weight_sem.at[0]),
        pltpu.make_async_copy(up_hbm, wgu.at[:, pl.ds(ff, ff)], weight_sem.at[1]),
        pltpu.make_async_copy(down_hbm, wd, weight_sem.at[2]),
    ]
    for load in loads:
        load.start()
    cy = 4 * c + y
    for p in range(panels):
        tok[p, cy, zl] = tokens[pl.ds(p * r, r), :]
    pl.semaphore_wait(barrier, len(peers))

    sent = []

    def send(p, name, src, dst, to):
        copy = pltpu.make_async_remote_copy(
            src_ref=src, dst_ref=dst, send_sem=send_sem.at[p, SEM[name]],
            recv_sem=recv_sem.at[p, SEM[name]], device_id=to, device_id_type=pl.DeviceIdType.MESH,
        )
        copy.start()
        sent.append(copy)

    def arrived(p, name, dst):
        pltpu.make_async_remote_copy(
            src_ref=dst, dst_ref=dst, send_sem=send_sem.at[p, SEM[name]],
            recv_sem=recv_sem.at[p, SEM[name]], device_id=core, device_id_type=pl.DeviceIdType.MESH,
        ).wait_recv()

    g, u = pl.ds(0, ff), pl.ds(ff, ff)
    ca, cb = pl.ds(0, mid), pl.ds(mid, mid)

    def two(j):
        return pl.ds(2 * mod4(j), 2)

    def f32(v):
        return v.astype(F32)

    def a1(p):
        for k in (1, 2, 3):
            here = tok.at[p, cy, zl]
            send(p, "az%d" % k, here, here, zs[k])

    def a2(p):
        for k in (1, 2, 3):
            arrived(p, "az%d" % k, tok.at[p, cy, mod4(zl - k)])
        here = tok.at[p, cy]
        send(p, "ayr", here, here, yr)
        send(p, "ayl", here, here, yl)

    def a3(p):
        left, right = 4 * c + mod4(y - 1), 4 * c + mod4(y + 1)
        arrived(p, "ayr", tok.at[p, left])
        here = tok.at[p, left, pl.ds(0, 2)]
        send(p, "arr", here, here, yr)
        arrived(p, "ayl", tok.at[p, right])
        here = tok.at[p, right, pl.ds(2, 2)]
        send(p, "arl", here, here, yl)

    def a4(p):
        far = 4 * c + mod4(y + 2)
        arrived(p, "arr", tok.at[p, far, pl.ds(0, 2)])
        arrived(p, "arl", tok.at[p, far, pl.ds(2, 2)])
        here = tok.at[p, pl.ds(4 * c, 4)]
        send(p, "ac", here, here, core)

    def m1(p):
        arrived(p, "ac", tok.at[p, pl.ds(4 * (1 - c), 4)])
        if p == 0:
            loads[0].wait()
            loads[1].wait()

        def tile(i, carry):
            columns = pl.ds(pl.multiple_of(i * 256, 256), 256)
            lhs = tok[p].reshape(8 * rows, tok.shape[-1])
            product = jnp.dot(lhs, wgu[:, columns], preferred_element_type=F32)
            part[p, :, :, columns] = product.astype(BF16).reshape(8, rows, 256)
            return carry

        lax.fori_loop(0, 2 * ff // 256, tile, 0)
        send(p, "s1g", part.at[p, two(x + 2), :, g], s1g.at[p], xr)
        send(p, "s1u", part.at[p, two(x + 2), :, u], s1u.at[p], xl)
        send(p, "sug", part.at[p, two(x + 1), :, u], sug.at[p], xr)
        send(p, "sgu", part.at[p, two(x - 1), :, g], sgu.at[p], xl)

    def x2(p):
        arrived(p, "s1g", s1g.at[p])
        part[p, two(x + 1), :, g] = (f32(part[p, two(x + 1), :, g]) + f32(s1g[p])).astype(BF16)
        send(p, "lg", part.at[p, two(x + 1), :, g], lg.at[p], xr)
        arrived(p, "s1u", s1u.at[p])
        part[p, two(x - 1), :, u] = (f32(part[p, two(x - 1), :, u]) + f32(s1u[p])).astype(BF16)
        send(p, "lu", part.at[p, two(x - 1), :, u], lu.at[p], xl)

    def z1(p):
        arrived(p, "lg", lg.at[p])
        arrived(p, "sgu", sgu.at[p])
        arrived(p, "lu", lu.at[p])
        arrived(p, "sug", sug.at[p])

        def total(b, cols, long, short):
            return f32(part[p, 2 * x + b, :, cols]) + f32(long[p, b]) + f32(short[p, b])

        zsend[p, :, g] = total(1 - h, g, lg, sgu).astype(BF16)
        zsend[p, :, u] = total(1 - h, u, lu, sug).astype(BF16)
        send(p, "z", zsend.at[p], zrecv.at[p], zpeer)
        zkeep[p, :, g] = total(h, g, lg, sgu)
        zkeep[p, :, u] = total(h, u, lu, sug)

    def hidden(p):
        arrived(p, "z", zrecv.at[p])
        gate = zkeep[p, :, g] + f32(zrecv[p, :, g])
        up = zkeep[p, :, u] + f32(zrecv[p, :, u])
        mine = 2 * x + h
        hid[p, mine] = (jax.nn.silu(gate) * up).astype(BF16)
        here = hid.at[p, mine]
        send(p, "ez", here, here, zpeer)
        send(p, "eor", here, here, xr)
        send(p, "eol", here, here, xl)

    def e2(p):
        here = hid.at[p, 2 * x + 1 - h]
        arrived(p, "ez", here)
        send(p, "epr", here, here, xr)
        send(p, "epl", here, here, xl)

    def e3(p):
        here = hid.at[p, 2 * mod4(x - 1) + h]
        arrived(p, "eor", here)
        send(p, "err", here, here, xr)
        here = hid.at[p, 2 * mod4(x + 1) + 1 - h]
        arrived(p, "epl", here)
        send(p, "erl", here, here, xl)

    def m2(p):
        arrived(p, "eol", hid.at[p, 2 * mod4(x + 1) + h])
        arrived(p, "epr", hid.at[p, 2 * mod4(x - 1) + 1 - h])
        arrived(p, "err", hid.at[p, 2 * mod4(x + 2) + h])
        arrived(p, "erl", hid.at[p, 2 * mod4(x + 2) + 1 - h])
        if p == 0:
            loads[2].wait()

        def tile(i, carry):
            columns = pl.ds(pl.multiple_of(i * 256, 256), 256)
            lhs = hid[p].reshape(8 * rows, ff)
            product = jnp.dot(lhs, wd[:, columns], preferred_element_type=F32)
            outp[p, :, :, columns] = product.astype(BF16).reshape(8, rows, 256)
            return carry

        lax.fori_loop(0, 2 * mid // 256, tile, 0)
        send(p, "gc", outp.at[p, pl.ds(4 * (1 - c), 4)], crecv.at[p], core)

    def g2(p):
        arrived(p, "gc", crecv.at[p])
        osum[p] = (f32(outp[p, pl.ds(4 * c, 4)]) + f32(crecv[p])).astype(BF16)
        send(p, "y1a", osum.at[p, mod4(y + 2), :, ca], y1a.at[p], yr)
        send(p, "y1b", osum.at[p, mod4(y + 2), :, cb], y1b.at[p], yl)
        send(p, "ysb", osum.at[p, mod4(y + 1), :, cb], ysb.at[p], yr)
        send(p, "ysa", osum.at[p, mod4(y - 1), :, ca], ysa.at[p], yl)

    def g3(p):
        arrived(p, "y1a", y1a.at[p])
        there = mod4(y + 1)
        osum[p, there, :, ca] = (f32(osum[p, there, :, ca]) + f32(y1a[p])).astype(BF16)
        send(p, "yla", osum.at[p, there, :, ca], yla.at[p], yr)
        arrived(p, "y1b", y1b.at[p])
        there = mod4(y - 1)
        osum[p, there, :, cb] = (f32(osum[p, there, :, cb]) + f32(y1b[p])).astype(BF16)
        send(p, "ylb", osum.at[p, there, :, cb], ylb.at[p], yl)

    def g4(p):
        arrived(p, "yla", yla.at[p])
        arrived(p, "ysa", ysa.at[p])
        arrived(p, "ylb", ylb.at[p])
        arrived(p, "ysb", ysb.at[p])
        a = f32(osum[p, y, :, ca]) + f32(yla[p]) + f32(ysa[p])
        b = f32(osum[p, y, :, cb]) + f32(ylb[p]) + f32(ysb[p])
        zos[p, :, :, ca] = a.astype(BF16).reshape(4, r, mid)
        zos[p, :, :, cb] = b.astype(BF16).reshape(4, r, mid)
        for k in (1, 2, 3):
            send(p, "gz%d" % k, zos.at[p, mod4(zl + k)], zor.at[p, k - 1], zs[k])

    def g5(p):
        total = f32(zos[p, zl])
        for k in (1, 2, 3):
            arrived(p, "gz%d" % k, zor.at[p, k - 1])
            total = total + f32(zor[p, k - 1])
        out[pl.ds(p * r, r), :] = total.astype(BF16)

    steps = dict(zip(STEPS, (a1, a2, a3, a4, m1, x2, z1, hidden, e2, e3, m2, g2, g3, g4, g5)))
    for p, step in step_order(panels):
        steps[step](p)
    for copy in sent:
        copy.wait_send()


def shards(tokens, gate_weight, up_weight, down_weight):
    n = PANELS
    r = 64 // n
    rows = 4 * r
    depth, ff = gate_weight.shape
    wide = down_weight.shape[1]
    vmem = pltpu.VMEM
    scratch = [
        vmem((depth, 2 * ff), BF16),
        vmem((ff, wide), BF16),
        vmem((n, 8, 4, r, depth), BF16),
        vmem((n, 8, rows, 2 * ff), BF16),
    ]
    scratch += [vmem((n, 2, rows, ff), BF16)] * 6
    scratch += [
        vmem((n, rows, 2 * ff), BF16),
        vmem((n, rows, 2 * ff), F32),
        vmem((n, rows, 2 * ff), BF16),
        vmem((n, 8, rows, ff), BF16),
        vmem((n, 8, rows, wide), BF16),
        vmem((n, 4, rows, wide), BF16),
        vmem((n, 4, rows, wide), BF16),
    ]
    scratch += [vmem((n, rows, wide // 2), BF16)] * 6
    scratch += [
        vmem((n, 4, r, wide), BF16),
        vmem((n, 3, r, wide), BF16),
        pltpu.SemaphoreType.DMA((n, len(COPIES))),
        pltpu.SemaphoreType.DMA((n, len(COPIES))),
        pltpu.SemaphoreType.DMA((3,)),
    ]
    whole = pl.BlockSpec(memory_space=pltpu.VMEM)
    anywhere = pl.BlockSpec(memory_space=pl.ANY)
    return pl.pallas_call(
        functools.partial(kernel, n),
        out_shape=jax.ShapeDtypeStruct(tokens.shape, BF16),
        in_specs=[whole, anywhere, anywhere, anywhere],
        out_specs=whole,
        scratch_shapes=scratch,
        compiler_params=pltpu.CompilerParams(
            collective_id=0, has_side_effects=True, vmem_limit_bytes=60 << 20
        ),
        name="swiglu",
    )(tokens, gate_weight, up_weight, down_weight)


def solution(mesh):
    return jax.shard_map(
        shards,
        mesh=mesh,
        in_specs=(
            P(("gx", "gy"), "gz"),
            P("gz", ("gx", "gy")),
            P("gz", ("gx", "gy")),
            P(("gx", "gy"), "gz"),
        ),
        out_specs=P(("gx", "gy"), "gz"),
        check_vma=False,
    )
```

```python
import jax
import jax.numpy as jnp
from jax import lax
from jax.experimental import pallas as pl
from jax.experimental.pallas import tpu as pltpu
from jax.sharding import PartitionSpec as P

PANELS = ((0, 0), (1, 0), (3, 0), (2, 0), (1, 1), (3, 1), (2, 1), (0, 1))
BF16, F32 = jnp.bfloat16, jnp.float32
ORDER = (
    ("A2", 0), ("A3", 0), ("A2", 1), ("A4", 0), ("A3", 1), ("A2", 3), ("M1", 0), ("A4", 1),
    ("A3", 3), ("A2", 4), ("A2", 2), ("M1", 1), ("A4", 3), ("X2", 0), ("A2", 6), ("A2", 7),
    ("A3", 4), ("A3", 2), ("M1", 3), ("X2", 1), ("A4", 2), ("A3", 6), ("A2", 5), ("Z1", 0),
    ("M1", 2), ("X2", 3), ("A3", 5), ("A4", 4), ("Z1", 1), ("A4", 5), ("A3", 7), ("A4", 6),
    ("H", 0), ("M1", 4), ("X2", 2), ("Z1", 3), ("M1", 5), ("X2", 4), ("H", 1), ("Z1", 2),
    ("E1", 0), ("X2", 5), ("H", 3), ("A4", 7), ("E2", 0), ("M1", 6), ("Z1", 4), ("M1", 7),
    ("Z1", 5), ("E3", 0), ("H", 2), ("H", 4), ("X2", 6), ("X2", 7), ("H", 5), ("E1", 1),
    ("M2", 0), ("Z1", 6), ("E2", 1), ("E1", 2), ("E2", 2), ("E1", 3), ("E3", 1), ("E2", 3),
    ("Z1", 7), ("E3", 2), ("E1", 4), ("E2", 4), ("H", 6), ("E1", 5), ("G2", 0), ("M2", 1),
    ("E3", 3), ("E2", 5), ("H", 7), ("G2", 1), ("E3", 4), ("E1", 6), ("M2", 2), ("E2", 6),
    ("M2", 3), ("E3", 5), ("E1", 7), ("G2", 2), ("M2", 4), ("E2", 7), ("G4", 1), ("E3", 6),
    ("G2", 3), ("G2", 4), ("M2", 5), ("E3", 7), ("G4", 2), ("M2", 6), ("G2", 5), ("G2", 6),
    ("M2", 7), ("G4", 0), ("G4", 3), ("G4", 4), ("G2", 7), ("G4", 5), ("G4", 6), ("G4", 7),
)
ARRIVALS = ("az", "ay", "ar", "ac", "s1", "lo", "z", "ez", "e1", "e2", "gc", "gy")
SENDS = ("tokens", "sums", "hidden", "outputs")


def kernel(
    tokens, gate_hbm, up_hbm, down_hbm, out,
    wgu, wd, tok, part, first, second, zsend, zkeep, zrecv, hid, outp,
    crecv, osum, ysum, zos, zown, zor, send_sem, recv_sem, last_sem, weight_sem,
):
    gx, gy, gz = lax.axis_index("gx"), lax.axis_index("gy"), lax.axis_index("gz")
    x, h, y, c, zl = lax.rem(gz, 4), gz // 4, gx // 2, lax.rem(gx, 2), gy
    rows = tok.shape[2]
    ff = gate_hbm.shape[1]

    def mod4(v):
        return lax.rem(v + 4, 4)

    def device(x=x, h=h, y=y, c=c, zl=zl):
        return {"gx": 2 * y + c, "gy": zl, "gz": 4 * h + x}

    xr, xl = device(x=mod4(x + 1)), device(x=mod4(x - 1))
    yr, yl, yf = device(y=mod4(y + 1)), device(y=mod4(y - 1)), device(y=mod4(y + 2))
    zpeer = device(h=1 - h)
    core = device(c=1 - c)
    zup = [None] + [device(zl=mod4(zl + k)) for k in (1, 2, 3)]
    zdown = [None, zup[3], zup[2], zup[1]]

    barrier = pltpu.get_barrier_semaphore()
    peers = (xr, xl, yr, yl, yf, zpeer, core, zup[1], zup[2], zup[3])
    for peer in peers:
        pl.semaphore_signal(barrier, inc=1, device_id=peer, device_id_type=pl.DeviceIdType.MESH)
    loads = [
        pltpu.make_async_copy(gate_hbm, wgu.at[:, pl.ds(0, ff)], weight_sem.at[0]),
        pltpu.make_async_copy(up_hbm, wgu.at[:, pl.ds(ff, ff)], weight_sem.at[1]),
        pltpu.make_async_copy(down_hbm, wd, weight_sem.at[2]),
    ]
    for load in loads:
        load.start()
    cy = 4 * c + y
    for p, (offset, q) in enumerate(PANELS):
        if offset == 0:
            tok[p, cy] = tokens[pl.ds(q * rows, rows), :]
    pl.semaphore_wait(barrier, len(peers))

    def send(p, group, name, src, dst, to):
        arrival = recv_sem.at[p, ARRIVALS.index(name)] if name in ARRIVALS else last_sem.at[PANELS[p][1]]
        pltpu.make_async_remote_copy(
            src_ref=src, dst_ref=dst, send_sem=send_sem.at[p, SENDS.index(group)],
            recv_sem=arrival, device_id=to, device_id_type=pl.DeviceIdType.MESH,
        ).start()

    def arrived(p, name, extent):
        arrival = recv_sem.at[p, ARRIVALS.index(name)] if name in ARRIVALS else last_sem.at[p]
        pltpu.make_async_remote_copy(
            src_ref=extent, dst_ref=extent, send_sem=send_sem.at[0, 0],
            recv_sem=arrival, device_id=core, device_id_type=pl.DeviceIdType.MESH,
        ).wait_recv()

    def flush(p):
        blocks = 8 if PANELS[p][0] else 7
        extents = (
            tok.at[p, pl.ds(0, blocks)], part.at[p, pl.ds(0, 7)],
            hid.at[p, pl.ds(0, 7)], outp.at[p, pl.ds(0, blocks)],
        )
        for i, extent in enumerate(extents):
            pltpu.make_async_remote_copy(
                src_ref=extent, dst_ref=extent, send_sem=send_sem.at[p, i],
                recv_sem=recv_sem.at[0, 0], device_id=core, device_id_type=pl.DeviceIdType.MESH,
            ).wait_send()

    g, u = pl.ds(0, ff), pl.ds(ff, ff)

    def two(j):
        return pl.ds(2 * mod4(j), 2)

    def f32(v):
        return v.astype(F32)

    def a1(p):
        offset, q = PANELS[p]
        if offset:
            send(p, "tokens", "az", tokens.at[pl.ds(q * rows, rows)], tok.at[p, cy], zdown[offset])

    def a2(p):
        here = tok.at[p, cy]
        if PANELS[p][0]:
            arrived(p, "az", here)
        send(p, "tokens", "ay", here, here, yr)
        send(p, "tokens", "ay", here, here, yl)

    def a3(p):
        arrived(p, "ay", tok.at[p, pl.ds(0, 2)])
        here = tok.at[p, 4 * c + mod4(y - 1), pl.ds(0, rows // 2)]
        send(p, "tokens", "ar", here, here, yr)
        here = tok.at[p, 4 * c + mod4(y + 1), pl.ds(rows // 2, rows // 2)]
        send(p, "tokens", "ar", here, here, yl)

    def a4(p):
        arrived(p, "ar", tok.at[p, 0])
        here = tok.at[p, pl.ds(4 * c, 4)]
        send(p, "tokens", "ac", here, here, core)

    def m1(p):
        arrived(p, "ac", tok.at[p, pl.ds(0, 4)])
        if p == 0:
            loads[0].wait()
            loads[1].wait()

        def tile(i, carry):
            columns = pl.ds(pl.multiple_of(i * 256, 256), 256)
            lhs = tok[p].reshape(8 * rows, tok.shape[-1])
            product = jnp.dot(lhs, wgu[:, columns], preferred_element_type=F32)
            part[p, :, :, columns] = product.astype(BF16).reshape(8, rows, 256)
            return carry

        tiles = 2 * ff // 256
        lax.fori_loop(0, (tiles + 1) // 2, tile, 0)
        send(p, "sums", "s1", part.at[p, two(x + 2), :, g], first.at[p, 0], xr)
        send(p, "sums", "lo", part.at[p, two(x - 1), :, g], second.at[p, 1], xl)
        lax.fori_loop((tiles + 1) // 2, tiles, tile, 0)
        send(p, "sums", "s1", part.at[p, two(x + 2), :, u], first.at[p, 1], xl)
        send(p, "sums", "lo", part.at[p, two(x + 1), :, u], second.at[p, 3], xr)

    def x2(p):
        arrived(p, "s1", first.at[p])
        there = two(x + 1)
        part[p, there, :, g] = (f32(part[p, there, :, g]) + f32(first[p, 0])).astype(BF16)
        send(p, "sums", "lo", part.at[p, there, :, g], second.at[p, 0], xr)
        there = two(x - 1)
        part[p, there, :, u] = (f32(part[p, there, :, u]) + f32(first[p, 1])).astype(BF16)
        send(p, "sums", "lo", part.at[p, there, :, u], second.at[p, 2], xl)

    def z1(p):
        arrived(p, "lo", second.at[p])

        def total(b, cols, i):
            return f32(part[p, 2 * x + b, :, cols]) + f32(second[p, i, b]) + f32(second[p, i + 1, b])

        zsend[p, :, g] = total(1 - h, g, 0).astype(BF16)
        zsend[p, :, u] = total(1 - h, u, 2).astype(BF16)
        send(p, "sums", "z", zsend.at[p], zrecv.at[p], zpeer)
        zkeep[p, :, g] = total(h, g, 0)
        zkeep[p, :, u] = total(h, u, 2)

    def hidden(p):
        arrived(p, "z", zrecv.at[p])
        gate = zkeep[p, :, g] + f32(zrecv[p, :, g])
        up = zkeep[p, :, u] + f32(zrecv[p, :, u])
        mine = 2 * x + h
        hid[p, mine] = (jax.nn.silu(gate) * up).astype(BF16)
        here = hid.at[p, mine]
        send(p, "hidden", "ez", here, here, zpeer)

    def e1(p):
        here = hid.at[p, 2 * x + h]
        send(p, "hidden", "e1", here, here, xr)
        send(p, "hidden", "e2", here, here, xl)

    def e2(p):
        here = hid.at[p, 2 * x + 1 - h]
        arrived(p, "ez", here)
        send(p, "hidden", "e1", here, here, xl)
        send(p, "hidden", "e2", here, here, xr)

    def e3(p):
        arrived(p, "e1", hid.at[p, pl.ds(0, 2)])
        here = hid.at[p, 2 * mod4(x - 1) + h]
        send(p, "hidden", "e2", here, here, xr)
        here = hid.at[p, 2 * mod4(x + 1) + 1 - h]
        send(p, "hidden", "e2", here, here, xl)

    def m2(p):
        arrived(p, "e2", hid.at[p, pl.ds(0, 4)])
        if p == 0:
            loads[2].wait()

        def tile(i, carry):
            columns = pl.ds(pl.multiple_of(i * 256, 256), 256)
            lhs = hid[p].reshape(8 * rows, ff)
            product = jnp.dot(lhs, wd[:, columns], preferred_element_type=F32)
            outp[p, :, :, columns] = product.astype(BF16).reshape(8, rows, 256)
            return carry

        lax.fori_loop(0, wd.shape[1] // 256, tile, 0)
        send(p, "outputs", "gc", outp.at[p, pl.ds(4 * (1 - c), 4)], crecv.at[p], core)

    def g2(p):
        if p == len(PANELS) - 1:
            g5(0)
        arrived(p, "gc", crecv.at[p])
        osum[p] = (f32(outp[p, pl.ds(4 * c, 4)]) + f32(crecv[p])).astype(BF16)
        send(p, "outputs", "gy", osum.at[p, mod4(y + 2)], ysum.at[p, 1], yf)
        send(p, "outputs", "gy", osum.at[p, mod4(y + 1)], ysum.at[p, 0], yr)
        send(p, "outputs", "gy", osum.at[p, mod4(y - 1)], ysum.at[p, 2], yl)

    def g4(p):
        offset, q = PANELS[p]
        arrived(p, "gy", ysum.at[p])
        total = f32(osum[p, y]) + f32(ysum[p, 0]) + f32(ysum[p, 1]) + f32(ysum[p, 2])
        if offset == 0:
            zown[q] = total
        else:
            zos[p] = total.astype(BF16)
            send(p, "outputs", "gz", zos.at[p], zor.at[q, offset - 1], zup[offset])

    def g5(q):
        arrived(q, "last", zor.at[q])
        total = zown[q] + f32(zor[q, 0]) + f32(zor[q, 1]) + f32(zor[q, 2])
        out[pl.ds(q * rows, rows), :] = total.astype(BF16)

    steps = dict(
        A2=a2, A3=a3, A4=a4, M1=m1, X2=x2, Z1=z1, H=hidden, E1=e1, E2=e2, E3=e3, M2=m2, G2=g2, G4=g4
    )
    steps[ORDER[0][0]](ORDER[0][1])
    for p in range(len(PANELS)):
        a1(p)
    for step, p in ORDER[1:]:
        steps[step](p)
    g5(1)
    for p in range(len(PANELS)):
        flush(p)


def shards(tokens, gate_weight, up_weight, down_weight):
    n = len(PANELS)
    rows = tokens.shape[0] // 2
    depth, ff = gate_weight.shape
    wide = down_weight.shape[1]
    vmem = pltpu.VMEM
    scratch = [
        vmem((depth, 2 * ff), BF16),
        vmem((ff, wide), BF16),
        vmem((n, 8, rows, depth), BF16),
        vmem((n, 8, rows, 2 * ff), BF16),
    ]
    scratch += [
        vmem((n, 2, 2, rows, ff), BF16),
        vmem((n, 4, 2, rows, ff), BF16),
        vmem((n, rows, 2 * ff), BF16),
        vmem((n, rows, 2 * ff), F32),
        vmem((n, rows, 2 * ff), BF16),
        vmem((n, 8, rows, ff), BF16),
        vmem((n, 8, rows, wide), BF16),
        vmem((n, 4, rows, wide), BF16),
        vmem((n, 4, rows, wide), BF16),
    ]
    scratch += [
        vmem((n, 3, rows, wide), BF16),
        vmem((n, rows, wide), BF16),
        vmem((2, rows, wide), F32),
        vmem((2, 3, rows, wide), BF16),
        pltpu.SemaphoreType.DMA((n, len(SENDS))),
        pltpu.SemaphoreType.DMA((n, len(ARRIVALS))),
        pltpu.SemaphoreType.DMA((2,)),
        pltpu.SemaphoreType.DMA((3,)),
    ]
    whole = pl.BlockSpec(memory_space=pltpu.VMEM)
    anywhere = pl.BlockSpec(memory_space=pl.ANY)
    return pl.pallas_call(
        kernel,
        out_shape=jax.ShapeDtypeStruct(tokens.shape, BF16),
        in_specs=[whole, anywhere, anywhere, anywhere],
        out_specs=whole,
        scratch_shapes=scratch,
        compiler_params=pltpu.CompilerParams(
            collective_id=0, has_side_effects=True, vmem_limit_bytes=60 << 20
        ),
        name="swiglu",
    )(tokens, gate_weight, up_weight, down_weight)


def solution(mesh):
    return jax.shard_map(
        shards,
        mesh=mesh,
        in_specs=(
            P(("gx", "gy"), "gz"),
            P("gz", ("gx", "gy")),
            P("gz", ("gx", "gy")),
            P(("gx", "gy"), "gz"),
        ),
        out_specs=P(("gx", "gy"), "gz"),
        check_vma=False,
    )
```

```python
import jax
import jax.numpy as jnp
from jax import lax
from jax.experimental import pallas as pl
from jax.experimental.pallas import tpu as pltpu
from jax.sharding import PartitionSpec as P

NEAR, MIDDLE, OWN = 0, 1, 10
SHIFTED = {
    2: (1, 0, 32), 3: (3, 0, 32), 4: (2, 0, 32), 5: (1, 32, 32),
    6: (3, 32, 16), 7: (3, 48, 16), 8: (2, 32, 16), 9: (2, 48, 16),
}
PANELS = 11
BIG, SMALL = (1, 2, 3, 4, 5), (0, 6, 7, 8, 9, 10)
BF16, F32 = jnp.bfloat16, jnp.float32
ORDER = (
    ("A2", 0), ("A2", 1), ("A2", 10), ("A4", 10), ("M1", 10), ("A4", 0), ("A2", 2), ("M1", 0),
    ("A4", 1), ("X2", 10), ("A2", 3), ("M1", 1), ("X2", 0), ("A2", 6), ("A2", 4), ("A4", 2),
    ("A2", 5), ("A4", 3), ("M1", 2), ("A4", 6), ("Z1", 10), ("X2", 1), ("A2", 7), ("A2", 9),
    ("A2", 8), ("Z1", 0), ("M1", 3), ("H", 0), ("A4", 4), ("A4", 7), ("A4", 9), ("A4", 5),
    ("X2", 2), ("Z1", 1), ("M1", 6), ("X2", 3), ("Z1", 2), ("M1", 7), ("H", 1), ("X2", 6),
    ("M1", 4), ("X2", 7), ("Z1", 3), ("M1", 5), ("Z1", 6), ("Z1", 7), ("X2", 4), ("A4", 8),
    ("H", 3), ("E1", 1), ("E2", 1), ("H", 2), ("X2", 5), ("M1", 8), ("Z1", 4), ("E3", 1),
    ("M1", 9), ("Z1", 5), ("E1", 3), ("X2", 8), ("H", 7), ("M2", 1), ("H", 4), ("E1", 2),
    ("E2", 2), ("E2", 3), ("X2", 9), ("Z1", 8), ("E1", 7), ("E3", 2), ("G2", 1), ("E1", 4),
    ("H", 5), ("E3", 3), ("E2", 7), ("E2", 4), ("Z1", 9), ("H", 6), ("M2", 2), ("E1", 5),
    ("H", 8), ("E2", 5), ("M2", 3), ("E3", 7), ("E3", 4), ("G2", 2), ("G4", 1), ("H", 9),
    ("E1", 6), ("E2", 6), ("H", 10), ("G2", 3), ("E3", 5), ("E1", 8), ("M2", 7), ("E2", 8),
    ("M2", 4), ("E3", 6), ("E1", 9), ("E2", 9), ("E1", 0), ("G2", 7), ("M2", 5), ("G2", 4),
    ("E3", 8), ("G4", 2), ("E2", 0), ("M2", 6), ("E3", 9), ("E1", 10), ("E2", 10), ("G2", 5),
    ("M2", 8), ("E3", 0), ("G2", 6), ("M2", 9), ("E3", 10), ("G4", 7), ("G2", 8), ("G4", 4),
    ("M2", 0), ("G2", 9), ("G4", 3), ("G4", 5), ("G4", 6), ("G2", 0), ("G4", 8), ("G4", 9),
    ("M2", 10), ("G2", 10), ("G4", 10), ("G4", 0),
)
FIRST_UP = next(p for step, p in ORDER if step == "M1")
FIRST_DOWN = next(p for step, p in ORDER if step == "M2")
ARRIVALS = ("az", "ay", "ac", "s1", "lo", "z", "ez", "e1", "e2", "gc", "gy")
SENDS = ("tokens", "sums", "hidden", "outputs")
BUFFERS = (
    "tok", "part", "first", "second", "zsend", "zkeep", "zrecv", "hid", "outp", "crecv", "osum", "ysum", "zos"
)


def buffers(panels, tall, depth, ff, wide):
    rows = tall[0] * tall[-1] if len(tall) > 1 else tall[0]
    shapes = (
        (8,) + tall + (depth,), (8, rows, 2 * ff), (2, 2, rows, ff), (4, 2, rows, ff), (rows, 2 * ff),
        (rows, 2 * ff), (rows, 2 * ff), (8, rows, ff), (8, rows, wide), (4, rows, wide),
        (4, rows, wide), (4, rows, wide), (rows, wide),
    )
    return [
        pltpu.VMEM((panels,) + shape, F32 if name == "zkeep" else BF16)
        for name, shape in zip(BUFFERS, shapes)
    ]


def kernel(tokens_hbm, gate_hbm, up_hbm, down_hbm, out, tokens, wgu, wd, total, zor, *scratch):
    big = dict(zip(BUFFERS, scratch))
    small = dict(zip(BUFFERS, scratch[len(BUFFERS):]))
    send_sem, recv_sem, last_sem, weight_sem = scratch[2 * len(BUFFERS):]
    gx, gy, gz = lax.axis_index("gx"), lax.axis_index("gy"), lax.axis_index("gz")
    x, h, y, c, zl = lax.rem(gz, 4), gz // 4, gx // 2, lax.rem(gx, 2), gy
    ff = gate_hbm.shape[1]

    def panel(p, name):
        group, members = (big, BIG) if p in BIG else (small, SMALL)
        return group[name].at[members.index(p)]

    def mod4(v):
        return lax.rem(v + 4, 4)

    def device(x=x, h=h, y=y, c=c, zl=zl):
        return {"gx": 2 * y + c, "gy": zl, "gz": 4 * h + x}

    xr, xl = device(x=mod4(x + 1)), device(x=mod4(x - 1))
    yr, yl, yf = device(y=mod4(y + 1)), device(y=mod4(y - 1)), device(y=mod4(y + 2))
    zpeer = device(h=1 - h)
    core = device(c=1 - c)
    zup = [None] + [device(zl=mod4(zl + k)) for k in (1, 2, 3)]
    zdown = [None, zup[3], zup[2], zup[1]]

    loads = [
        pltpu.make_async_copy(tokens_hbm, tokens, weight_sem.at[3]),
        pltpu.make_async_copy(gate_hbm, wgu.at[:, pl.ds(0, ff)], weight_sem.at[0]),
        pltpu.make_async_copy(up_hbm, wgu.at[:, pl.ds(ff, ff)], weight_sem.at[1]),
        pltpu.make_async_copy(down_hbm, wd, weight_sem.at[2]),
    ]
    barrier = pltpu.get_barrier_semaphore()
    peers = (xr, xl, yr, yl, yf, zpeer, core, zup[1], zup[2], zup[3])
    for peer in peers:
        pl.semaphore_signal(barrier, inc=1, device_id=peer, device_id_type=pl.DeviceIdType.MESH)
    for load in loads:
        load.start()
    cy = 4 * c + y
    total[...] = jnp.zeros_like(total)
    loads[0].wait()
    pl.semaphore_wait(barrier, len(peers))

    def arrival(p, name):
        return recv_sem.at[p, ARRIVALS.index(name)] if name in ARRIVALS else last_sem.at[p]

    def send(p, group, name, src, dst, to):
        pltpu.make_async_remote_copy(
            src_ref=src, dst_ref=dst, send_sem=send_sem.at[2 if p == OWN else int(p in SMALL), SENDS.index(group)],
            recv_sem=arrival(SHIFTED[p][1] // 32 if name == "last" else p, name),
            device_id=to, device_id_type=pl.DeviceIdType.MESH,
        ).start()

    def arrived(p, name, extent):
        pltpu.make_async_remote_copy(
            src_ref=extent, dst_ref=extent, send_sem=send_sem.at[0, 0],
            recv_sem=arrival(p, name), device_id=core, device_id_type=pl.DeviceIdType.MESH,
        ).wait_recv()

    def flush():
        for i, name in enumerate(("tok", "part", "hid", "outp")):
            whole = name in ("tok", "outp")
            blocks = pl.ds(0, 8 if whole else 7)
            extents = (
                big[name].at[:, blocks], small[name].at[pl.ds(0, 5), blocks],
                small[name].at[5, pl.ds(0, 4 if whole else 7)],
            )
            for k, extent in enumerate(extents):
                pltpu.make_async_remote_copy(
                    src_ref=extent, dst_ref=extent, send_sem=send_sem.at[k, i],
                    recv_sem=recv_sem.at[0, 0], device_id=core, device_id_type=pl.DeviceIdType.MESH,
                ).wait_send()

    g, u = pl.ds(0, ff), pl.ds(ff, ff)

    def two(j):
        return pl.ds(2 * mod4(j), 2)

    def f32(v):
        return v.astype(F32)

    upper, lower = pl.ds(0, 2), pl.ds(2, 2)

    def a1(p):
        offset, row, rows = SHIFTED[p]
        source = tokens.at[pl.ds(row // 16, 2)] if rows == 32 else tokens.at[row // 16]
        send(p, "tokens", "az", source, panel(p, "tok").at[cy], zdown[offset])

    def a2(p):
        tok = panel(p, "tok")
        if p == OWN:
            tok[pl.ds(4 * c, 4)] = tokens[...]
        elif p == NEAR:
            send(p, "tokens", "ay", tokens.at[upper], tok.at[pl.ds(4 * c + 2, 2)], yr)
            send(p, "tokens", "ay", tokens.at[upper], tok.at[pl.ds(4 * c, 2)], yl)
        elif p == MIDDLE:
            send(p, "tokens", "ay", tokens.at[lower], tok.at[4 * c + 1], yr)
            send(p, "tokens", "ay", tokens.at[lower], tok.at[4 * c], yl)
            send(p, "tokens", "ay", tokens.at[upper], tok.at[4 * c + 2], yf)
            send(p, "tokens", "ay", tokens.at[lower], tok.at[4 * c + 3], yf)
        else:
            here = tok.at[cy]
            arrived(p, "az", here)
            send(p, "tokens", "ay", here, here, yf)
            send(p, "tokens", "ay", here, here, yr)
            send(p, "tokens", "ay", here, here, yl)

    def a4(p):
        tok = panel(p, "tok")
        if p != OWN:
            arrived(p, "ay", tok.at[pl.ds(0, 3 if p in SHIFTED else 4)])
        here = tok.at[pl.ds(4 * c, 4)]
        send(p, "tokens", "ac", here, here, core)

    def m1(p):
        tok, part, first, second = (panel(p, n) for n in ("tok", "part", "first", "second"))
        arrived(p, "ac", tok.at[pl.ds(0, 4)])
        if p == FIRST_UP:
            loads[1].wait()
            loads[2].wait()
        rows = part.shape[1]

        def tile(i, carry):
            columns = pl.ds(pl.multiple_of(i * 256, 256), 256)
            lhs = tok[...].reshape(8 * rows, tok.shape[-1])
            product = jnp.dot(lhs, wgu[:, columns], preferred_element_type=F32)
            part[:, :, columns] = product.astype(BF16).reshape(8, rows, 256)
            return carry

        tiles = 2 * ff // 256
        lax.fori_loop(0, (tiles + 1) // 2, tile, 0)
        send(p, "sums", "s1", part.at[two(x + 2), :, g], first.at[0], xr)
        send(p, "sums", "lo", part.at[two(x - 1), :, g], second.at[1], xl)
        lax.fori_loop((tiles + 1) // 2, tiles, tile, 0)
        send(p, "sums", "s1", part.at[two(x + 2), :, u], first.at[1], xl)
        send(p, "sums", "lo", part.at[two(x + 1), :, u], second.at[3], xr)

    def x2(p):
        part, first, second = (panel(p, n) for n in ("part", "first", "second"))
        arrived(p, "s1", first)
        there = two(x + 1)
        part[there, :, g] = (f32(part[there, :, g]) + f32(first[0])).astype(BF16)
        send(p, "sums", "lo", part.at[there, :, g], second.at[0], xr)
        there = two(x - 1)
        part[there, :, u] = (f32(part[there, :, u]) + f32(first[1])).astype(BF16)
        send(p, "sums", "lo", part.at[there, :, u], second.at[2], xl)

    def z1(p):
        part, second = panel(p, "part"), panel(p, "second")
        zsend, zkeep, zrecv = (panel(p, n) for n in ("zsend", "zkeep", "zrecv"))
        arrived(p, "lo", second)

        def summed(b, cols, i):
            return f32(part[2 * x + b, :, cols]) + f32(second[i, b]) + f32(second[i + 1, b])

        zsend[:, g] = summed(1 - h, g, 0).astype(BF16)
        zsend[:, u] = summed(1 - h, u, 2).astype(BF16)
        send(p, "sums", "z", zsend, zrecv, zpeer)
        zkeep[:, g] = summed(h, g, 0)
        zkeep[:, u] = summed(h, u, 2)

    def hidden(p):
        hid, zkeep, zrecv = (panel(p, n) for n in ("hid", "zkeep", "zrecv"))
        arrived(p, "z", zrecv)
        gate = zkeep[:, g] + f32(zrecv[:, g])
        up = zkeep[:, u] + f32(zrecv[:, u])
        mine = 2 * x + h
        hid[mine] = (jax.nn.silu(gate) * up).astype(BF16)
        send(p, "hidden", "ez", hid.at[mine], hid.at[mine], zpeer)

    def e1(p):
        here = panel(p, "hid").at[2 * x + h]
        send(p, "hidden", "e1", here, here, xr)
        send(p, "hidden", "e2", here, here, xl)

    def e2(p):
        here = panel(p, "hid").at[2 * x + 1 - h]
        arrived(p, "ez", here)
        send(p, "hidden", "e1", here, here, xl)
        send(p, "hidden", "e2", here, here, xr)

    def e3(p):
        hid = panel(p, "hid")
        arrived(p, "e1", hid.at[pl.ds(0, 2)])
        here = hid.at[2 * mod4(x - 1) + h]
        send(p, "hidden", "e2", here, here, xr)
        here = hid.at[2 * mod4(x + 1) + 1 - h]
        send(p, "hidden", "e2", here, here, xl)

    def m2(p):
        hid, outp, crecv = (panel(p, n) for n in ("hid", "outp", "crecv"))
        arrived(p, "e2", hid.at[pl.ds(0, 4)])
        if p == FIRST_DOWN:
            loads[3].wait()
        rows = hid.shape[1]

        def tile(i, carry):
            columns = pl.ds(pl.multiple_of(i * 256, 256), 256)
            lhs = hid[...].reshape(8 * rows, ff)
            product = jnp.dot(lhs, wd[:, columns], preferred_element_type=F32)
            outp[:, :, columns] = product.astype(BF16).reshape(8, rows, 256)
            return carry

        lax.fori_loop(0, wd.shape[1] // 256, tile, 0)
        send(p, "outputs", "gc", outp.at[pl.ds(4 * (1 - c), 4)], crecv, core)

    def g2(p):
        outp, crecv, osum, ysum = (panel(p, n) for n in ("outp", "crecv", "osum", "ysum"))
        arrived(p, "gc", crecv)
        both = f32(outp[pl.ds(4 * c, 4)]) + f32(crecv[...])
        if p == OWN:
            total[...] += both.reshape(total.shape)
            return
        osum[...] = both.astype(BF16)
        if p == NEAR:
            send(p, "outputs", "gy", osum.at[upper], ysum.at[upper], yr)
            send(p, "outputs", "gy", osum.at[lower], ysum.at[lower], yl)
        elif p == MIDDLE:
            send(p, "outputs", "gy", osum.at[lower], ysum.at[lower], yf)
            send(p, "outputs", "gy", osum.at[0], ysum.at[0], yr)
            send(p, "outputs", "gy", osum.at[1], ysum.at[1], yl)
        else:
            send(p, "outputs", "gy", osum.at[mod4(y + 2)], ysum.at[1], yf)
            send(p, "outputs", "gy", osum.at[mod4(y + 1)], ysum.at[0], yr)
            send(p, "outputs", "gy", osum.at[mod4(y - 1)], ysum.at[2], yl)

    def g4(p):
        osum, ysum, zos = (panel(p, n) for n in ("osum", "ysum", "zos"))
        if p == NEAR:
            arrived(p, "gy", ysum)
            total[pl.ds(0, 32)] += (f32(ysum[upper]) + f32(ysum[lower])).reshape(32, total.shape[1])
        elif p == MIDDLE:
            arrived(p, "gy", ysum)
            total[pl.ds(0, 32)] += f32(ysum[2])
            total[pl.ds(32, 32)] += f32(ysum[0]) + f32(ysum[1]) + f32(ysum[3])
        elif p in SHIFTED:
            offset, row, rows = SHIFTED[p]
            arrived(p, "gy", ysum.at[pl.ds(0, 3)])
            zos[...] = (f32(osum[y]) + f32(ysum[0]) + f32(ysum[1]) + f32(ysum[2])).astype(BF16)
            there = zor.at[row // 32, offset - 1, pl.ds(row % 32, rows)]
            send(p, "outputs", "last", zos, there, zup[offset])

    def g5(q):
        arrived(q, "last", zor.at[q])
        rows = pl.ds(32 * q, 32)
        whole = total[rows] + f32(zor[q, 0]) + f32(zor[q, 1]) + f32(zor[q, 2])
        out[rows, :] = whole.astype(BF16)

    steps = dict(A2=a2, A4=a4, M1=m1, X2=x2, Z1=z1, H=hidden, E1=e1, E2=e2, E3=e3, M2=m2, G2=g2, G4=g4)
    steps[ORDER[0][0]](ORDER[0][1])
    for p in SHIFTED:
        a1(p)
    for step, p in ORDER[1:]:
        steps[step](p)
    g5(0)
    g5(1)
    flush()


def shards(tokens, gate_weight, up_weight, down_weight):
    depth, ff = gate_weight.shape
    quarters = tokens.reshape(4, 16, depth)
    wide = down_weight.shape[1]
    scratch = [
        pltpu.VMEM(quarters.shape, BF16),
        pltpu.VMEM((depth, 2 * ff), BF16),
        pltpu.VMEM((ff, wide), BF16),
        pltpu.VMEM(tokens.shape, F32),
        pltpu.VMEM((2, 3, 32, wide), BF16),
    ]
    scratch += buffers(len(BIG), (2, 16), depth, ff, wide) + buffers(len(SMALL), (16,), depth, ff, wide)
    scratch += [
        pltpu.SemaphoreType.DMA((3, len(SENDS))),
        pltpu.SemaphoreType.DMA((PANELS, len(ARRIVALS))),
        pltpu.SemaphoreType.DMA((2,)),
        pltpu.SemaphoreType.DMA((4,)),
    ]
    whole = pl.BlockSpec(memory_space=pltpu.VMEM)
    anywhere = pl.BlockSpec(memory_space=pl.ANY)
    return pl.pallas_call(
        kernel,
        out_shape=jax.ShapeDtypeStruct(tokens.shape, BF16),
        in_specs=[anywhere] * 4,
        out_specs=whole,
        scratch_shapes=scratch,
        compiler_params=pltpu.CompilerParams(
            collective_id=0, has_side_effects=True, vmem_limit_bytes=60 << 20
        ),
        name="swiglu",
    )(quarters, gate_weight, up_weight, down_weight)


def solution(mesh):
    return jax.shard_map(
        shards,
        mesh=mesh,
        in_specs=(
            P(("gx", "gy"), "gz"),
            P("gz", ("gx", "gy")),
            P("gz", ("gx", "gy")),
            P(("gx", "gy"), "gz"),
        ),
        out_specs=P(("gx", "gy"), "gz"),
        check_vma=False,
    )
```

```python
import jax
import jax.numpy as jnp
from jax import lax
from jax.experimental import pallas as pl
from jax.experimental.pallas import tpu as pltpu
from jax.sharding import PartitionSpec as P

NEAR, FAR, HERE, SHIFTED = range(4)
PANELS = (
    (NEAR, 0, 0, 16), (NEAR, 0, 32, 16), (FAR, 0, 0, 16),
    (SHIFTED, 1, 0, 32), (SHIFTED, 3, 0, 32), (SHIFTED, 2, 0, 16),
    (SHIFTED, 2, 16, 16), (SHIFTED, 1, 32, 16), (SHIFTED, 1, 48, 16),
    (SHIFTED, 3, 32, 16), (SHIFTED, 3, 48, 16), (SHIFTED, 2, 32, 16),
    (SHIFTED, 2, 48, 16), (HERE, 0, 0, 16),
)
KIND = tuple(panel[0] for panel in PANELS)
OWN = KIND.index(HERE)
BIG = tuple(p for p, panel in enumerate(PANELS) if panel[3] == 32)
SMALL = tuple(p for p, panel in enumerate(PANELS) if panel[3] == 16 and p != OWN) + (OWN,)
BF16, F32 = jnp.bfloat16, jnp.float32
A2, A4, M1, X2, Z1, H, E1, E2, E3, M2, G2, G4 = range(12)
ORDER = (
    (A2, 0), (A2, 1), (A2, 2), (A2, 13), (A4, 13), (M1, 13), (A4, 0), (A4, 1),
    (M1, 0), (A2, 3), (A2, 5), (X2, 13), (A4, 2), (M1, 1), (M1, 2), (A2, 6),
    (A4, 3), (X2, 0), (A2, 10), (A2, 4), (A2, 12), (X2, 1), (M1, 3), (X2, 2),
    (A4, 5), (A4, 6), (Z1, 0), (Z1, 13), (A4, 10), (M1, 5), (A4, 4), (X2, 3),
    (Z1, 1), (M1, 4), (A4, 12), (Z1, 2), (A2, 11), (A2, 7), (A2, 9), (Z1, 3),
    (A2, 8), (X2, 5), (A4, 11), (M1, 10), (H, 13), (X2, 4), (Z1, 5), (H, 2),
    (A4, 9), (M1, 6), (M1, 11), (X2, 10), (H, 3), (M1, 12), (Z1, 4), (X2, 11),
    (E1, 2), (H, 5), (X2, 6), (E2, 2), (E1, 5), (M1, 9), (Z1, 10), (A4, 8),
    (H, 4), (X2, 12), (M1, 8), (A4, 7), (Z1, 6), (X2, 9), (Z1, 11), (M1, 7),
    (H, 10), (Z1, 12), (E2, 5), (E1, 3), (X2, 8), (E2, 3), (H, 6), (E3, 2),
    (H, 11), (X2, 7), (Z1, 9), (Z1, 8), (E1, 4), (E3, 3), (E2, 4), (H, 12),
    (M2, 2), (Z1, 7), (E3, 5), (E1, 10), (E2, 10), (E1, 11), (E2, 11), (M2, 3),
    (G2, 2), (E3, 4), (H, 9), (E1, 12), (M2, 5), (E2, 12), (H, 8), (H, 0),
    (E3, 10), (E3, 11), (E1, 6), (G2, 3), (H, 7), (E2, 6), (E1, 9), (M2, 4),
    (E2, 9), (E1, 8), (G2, 5), (H, 1), (E3, 12), (M2, 10), (E2, 8), (M2, 11),
    (E3, 6), (G2, 4), (E1, 7), (E3, 9), (G2, 10), (E2, 7), (E1, 0), (E2, 0),
    (M2, 12), (G2, 11), (E3, 8), (E1, 1), (G4, 3), (M2, 6), (E2, 1), (G4, 2),
    (M2, 9), (E3, 7), (G2, 12), (E3, 0), (G4, 4), (E1, 13), (G2, 6), (M2, 8),
    (G2, 9), (E2, 13), (E3, 1), (G4, 10), (M2, 7), (G4, 5), (G2, 8), (M2, 0),
    (G4, 12), (G4, 11), (G2, 7), (E3, 13), (M2, 1), (G2, 0), (G4, 6), (G4, 9),
    (G2, 1), (G4, 8), (G4, 7), (M2, 13), (G2, 13), (G4, 13), (G4, 0), (G4, 1),
)
FIRST_UP = next(p for step, p in ORDER if step == M1)
FIRST_DOWN = next(p for step, p in ORDER if step == M2)
ARRIVALS = ("az", "ay", "ac", "s1", "lo", "z", "ez", "e1", "e2", "gc", "gy")
SENDS = ("tokens", "sums", "hidden", "outputs")
RECEIVE = {
    key: i for i, key in enumerate(
        [(p, name) for p, kind in enumerate(KIND) for name in ARRIVALS
         if not (name == "az" and kind != SHIFTED or name in ("ay", "gy") and kind == HERE)]
        + [(0, "last"), (1, "last")]
    )
}
BUFFERS = (
    "tok", "part", "first", "second", "zsend", "zkeep", "zrecv", "hid", "outp", "crecv", "osum", "ysum", "zos"
)


def buffers(panels, tall, depth, ff, wide):
    rows = tall[0] * tall[-1] if len(tall) > 1 else tall[0]
    shapes = (
        (8,) + tall + (depth,), (8, rows, 2 * ff), (2, 2, rows, ff), (4, 2, rows, ff), (rows, 2 * ff),
        (rows, 2 * ff), (rows, 2 * ff), (8, rows, ff), (8, rows, wide), (4, rows, wide),
        (4, rows, wide), (4, rows, wide), (rows, wide),
    )
    return [
        pltpu.VMEM((panels,) + shape, F32 if name == "zkeep" else BF16)
        for name, shape in zip(BUFFERS, shapes)
    ]


def kernel(tokens, gate_hbm, up_hbm, down_hbm, out, wgu, wd, total, zor, *scratch):
    big = dict(zip(BUFFERS, scratch))
    small = dict(zip(BUFFERS, scratch[len(BUFFERS):]))
    send_sem, recv_sem, weight_sem = scratch[2 * len(BUFFERS):]
    gx, gy, gz = lax.axis_index("gx"), lax.axis_index("gy"), lax.axis_index("gz")
    x, h, y, c, zl = lax.rem(gz, 4), gz // 4, gx // 2, lax.rem(gx, 2), gy
    ff = gate_hbm.shape[1]

    def panel(p, name):
        group, members = (big, BIG) if p in BIG else (small, SMALL)
        return group[name].at[members.index(p)]

    def mod4(v):
        return lax.rem(v + 4, 4)

    def device(x=x, h=h, y=y, c=c, zl=zl):
        return {"gx": 2 * y + c, "gy": zl, "gz": 4 * h + x}

    xr, xl = device(x=mod4(x + 1)), device(x=mod4(x - 1))
    yr, yl, yf = device(y=mod4(y + 1)), device(y=mod4(y - 1)), device(y=mod4(y + 2))
    zpeer = device(h=1 - h)
    core = device(c=1 - c)
    zup = [None] + [device(zl=mod4(zl + k)) for k in (1, 2, 3)]
    zdown = [None, zup[3], zup[2], zup[1]]

    loads = [
        pltpu.make_async_copy(tokens, panel(OWN, "tok").at[pl.ds(4 * c, 4)], weight_sem.at[3]),
        pltpu.make_async_copy(gate_hbm, wgu.at[:, pl.ds(0, ff)], weight_sem.at[0]),
        pltpu.make_async_copy(up_hbm, wgu.at[:, pl.ds(ff, ff)], weight_sem.at[1]),
        pltpu.make_async_copy(down_hbm, wd, weight_sem.at[2]),
    ]
    barrier = pltpu.get_barrier_semaphore()
    peers = (xr, xl, yr, yl, yf, zpeer, core, zup[1], zup[2], zup[3])
    for peer in peers:
        pl.semaphore_signal(barrier, inc=1, device_id=peer, device_id_type=pl.DeviceIdType.MESH)
    for load in loads:
        load.start()
    cy = 4 * c + y
    total[...] = jnp.zeros_like(total)
    pl.semaphore_wait(barrier, len(peers))

    def arrival(p, name):
        return recv_sem.at[RECEIVE[p, name]]

    def send(p, group, name, src, dst, to):
        pltpu.make_async_remote_copy(
            src_ref=src, dst_ref=dst, send_sem=send_sem.at[2 if p == OWN else int(p in SMALL), SENDS.index(group)],
            recv_sem=arrival(PANELS[p][2] // 32 if name == "last" else p, name),
            device_id=to, device_id_type=pl.DeviceIdType.MESH,
        ).start()

    def arrived(p, name, extent):
        pltpu.make_async_remote_copy(
            src_ref=extent, dst_ref=extent, send_sem=send_sem.at[0, 0],
            recv_sem=arrival(p, name), device_id=core, device_id_type=pl.DeviceIdType.MESH,
        ).wait_recv()

    def flush():
        for i, name in enumerate(("tok", "part", "hid", "outp")):
            whole = name in ("tok", "outp")
            blocks, others = pl.ds(0, 8 if whole else 7), len(SMALL) - 1
            extents = (
                big[name].at[:, blocks], small[name].at[pl.ds(0, others), blocks],
                small[name].at[others, pl.ds(0, 4 if whole else 7)],
            )
            for k, extent in enumerate(extents):
                pltpu.make_async_remote_copy(
                    src_ref=extent, dst_ref=extent, send_sem=send_sem.at[k, i],
                    recv_sem=recv_sem.at[0], device_id=core, device_id_type=pl.DeviceIdType.MESH,
                ).wait_send()

    g, u = pl.ds(0, ff), pl.ds(ff, ff)

    def two(j):
        return pl.ds(2 * mod4(j), 2)

    def f32(v):
        return v.astype(F32)

    upper, lower = pl.ds(0, 2), pl.ds(2, 2)

    def a1(p):
        _, offset, row, rows = PANELS[p]
        source = tokens.at[pl.ds(row // 16, 2)] if rows == 32 else tokens.at[row // 16]
        send(p, "tokens", "az", source, panel(p, "tok").at[cy], zdown[offset])

    def a2(p):
        tok = panel(p, "tok")
        if KIND[p] == HERE:
            loads[0].wait()
        elif KIND[p] == NEAR:
            mine = tokens.at[pl.ds(PANELS[p][2] // 16, 2)]
            send(p, "tokens", "ay", mine, tok.at[pl.ds(4 * c + 2, 2)], yr)
            send(p, "tokens", "ay", mine, tok.at[pl.ds(4 * c, 2)], yl)
        elif KIND[p] == FAR:
            send(p, "tokens", "ay", tokens, tok.at[pl.ds(4 * c, 4)], yf)
        else:
            here = tok.at[cy]
            arrived(p, "az", here)
            send(p, "tokens", "ay", here, here, yf)
            send(p, "tokens", "ay", here, here, yr)
            send(p, "tokens", "ay", here, here, yl)

    def a4(p):
        tok = panel(p, "tok")
        if p != OWN:
            arrived(p, "ay", tok.at[pl.ds(0, 3 if KIND[p] == SHIFTED else 4)])
        here = tok.at[pl.ds(4 * c, 4)]
        send(p, "tokens", "ac", here, here, core)

    def m1(p):
        tok, part, first, second = (panel(p, n) for n in ("tok", "part", "first", "second"))
        arrived(p, "ac", tok.at[pl.ds(0, 4)])
        if p == FIRST_UP:
            loads[1].wait()
            loads[2].wait()
        rows = part.shape[1]

        def tile(i, carry):
            columns = pl.ds(pl.multiple_of(i * 256, 256), 256)
            lhs = tok[...].reshape(8 * rows, tok.shape[-1])
            product = jnp.dot(lhs, wgu[:, columns], preferred_element_type=F32)
            part[:, :, columns] = product.astype(BF16).reshape(8, rows, 256)
            return carry

        tiles = 2 * ff // 256
        lax.fori_loop(0, (tiles + 1) // 2, tile, 0)
        send(p, "sums", "s1", part.at[two(x + 2), :, g], first.at[0], xr)
        send(p, "sums", "lo", part.at[two(x - 1), :, g], second.at[1], xl)
        lax.fori_loop((tiles + 1) // 2, tiles, tile, 0)
        send(p, "sums", "s1", part.at[two(x + 2), :, u], first.at[1], xl)
        send(p, "sums", "lo", part.at[two(x + 1), :, u], second.at[3], xr)

    def x2(p):
        part, first, second = (panel(p, n) for n in ("part", "first", "second"))
        arrived(p, "s1", first)
        there = two(x + 1)
        part[there, :, g] = (f32(part[there, :, g]) + f32(first[0])).astype(BF16)
        send(p, "sums", "lo", part.at[there, :, g], second.at[0], xr)
        there = two(x - 1)
        part[there, :, u] = (f32(part[there, :, u]) + f32(first[1])).astype(BF16)
        send(p, "sums", "lo", part.at[there, :, u], second.at[2], xl)

    def z1(p):
        part, second = panel(p, "part"), panel(p, "second")
        zsend, zkeep, zrecv = (panel(p, n) for n in ("zsend", "zkeep", "zrecv"))
        arrived(p, "lo", second)

        def summed(b, cols, i):
            return f32(part[2 * x + b, :, cols]) + f32(second[i, b]) + f32(second[i + 1, b])

        zsend[:, g] = summed(1 - h, g, 0).astype(BF16)
        zsend[:, u] = summed(1 - h, u, 2).astype(BF16)
        send(p, "sums", "z", zsend, zrecv, zpeer)
        zkeep[:, g] = summed(h, g, 0)
        zkeep[:, u] = summed(h, u, 2)

    def hidden(p):
        hid, zkeep, zrecv = (panel(p, n) for n in ("hid", "zkeep", "zrecv"))
        arrived(p, "z", zrecv)
        gate = zkeep[:, g] + f32(zrecv[:, g])
        up = zkeep[:, u] + f32(zrecv[:, u])
        mine = 2 * x + h
        hid[mine] = (jax.nn.silu(gate) * up).astype(BF16)
        send(p, "hidden", "ez", hid.at[mine], hid.at[mine], zpeer)

    def e1(p):
        here = panel(p, "hid").at[2 * x + h]
        send(p, "hidden", "e1", here, here, xr)
        send(p, "hidden", "e2", here, here, xl)

    def e2(p):
        here = panel(p, "hid").at[2 * x + 1 - h]
        arrived(p, "ez", here)
        send(p, "hidden", "e1", here, here, xl)
        send(p, "hidden", "e2", here, here, xr)

    def e3(p):
        hid = panel(p, "hid")
        arrived(p, "e1", hid.at[pl.ds(0, 2)])
        here = hid.at[2 * mod4(x - 1) + h]
        send(p, "hidden", "e2", here, here, xr)
        here = hid.at[2 * mod4(x + 1) + 1 - h]
        send(p, "hidden", "e2", here, here, xl)

    def m2(p):
        hid, outp, crecv = (panel(p, n) for n in ("hid", "outp", "crecv"))
        arrived(p, "e2", hid.at[pl.ds(0, 4)])
        if p == FIRST_DOWN:
            loads[3].wait()
        rows = hid.shape[1]

        def tile(i, carry):
            columns = pl.ds(pl.multiple_of(i * 256, 256), 256)
            lhs = hid[...].reshape(8 * rows, ff)
            product = jnp.dot(lhs, wd[:, columns], preferred_element_type=F32)
            outp[:, :, columns] = product.astype(BF16).reshape(8, rows, 256)
            return carry

        lax.fori_loop(0, wd.shape[1] // 256, tile, 0)
        send(p, "outputs", "gc", outp.at[pl.ds(4 * (1 - c), 4)], crecv, core)

    def g2(p):
        outp, crecv, osum, ysum = (panel(p, n) for n in ("outp", "crecv", "osum", "ysum"))
        arrived(p, "gc", crecv)
        both = f32(outp[pl.ds(4 * c, 4)]) + f32(crecv[...])
        if p == OWN:
            total[...] += both.reshape(total.shape)
            return
        osum[...] = both.astype(BF16)
        if KIND[p] == NEAR:
            send(p, "outputs", "gy", osum.at[upper], ysum.at[upper], yr)
            send(p, "outputs", "gy", osum.at[lower], ysum.at[lower], yl)
        elif KIND[p] == FAR:
            send(p, "outputs", "gy", osum, ysum, yf)
        else:
            send(p, "outputs", "gy", osum.at[mod4(y + 2)], ysum.at[1], yf)
            send(p, "outputs", "gy", osum.at[mod4(y + 1)], ysum.at[0], yr)
            send(p, "outputs", "gy", osum.at[mod4(y - 1)], ysum.at[2], yl)

    def g4(p):
        osum, ysum, zos = (panel(p, n) for n in ("osum", "ysum", "zos"))
        if KIND[p] == NEAR:
            arrived(p, "gy", ysum)
            rows = pl.ds(PANELS[p][2], 32)
            total[rows] += (f32(ysum[upper]) + f32(ysum[lower])).reshape(32, total.shape[1])
        elif KIND[p] == FAR:
            arrived(p, "gy", ysum)
            total[...] += f32(ysum[...]).reshape(total.shape)
        elif KIND[p] == SHIFTED:
            _, offset, row, rows = PANELS[p]
            arrived(p, "gy", ysum.at[pl.ds(0, 3)])
            zos[...] = (f32(osum[y]) + f32(ysum[0]) + f32(ysum[1]) + f32(ysum[2])).astype(BF16)
            there = zor.at[row // 32, offset - 1, pl.ds(row % 32, rows)]
            send(p, "outputs", "last", zos, there, zup[offset])

    def g5(q):
        arrived(q, "last", zor.at[q])
        rows = pl.ds(32 * q, 32)
        whole = total[rows] + f32(zor[q, 0]) + f32(zor[q, 1]) + f32(zor[q, 2])
        out[rows, :] = whole.astype(BF16)

    steps = (a2, a4, m1, x2, z1, hidden, e1, e2, e3, m2, g2, g4)
    steps[ORDER[0][0]](ORDER[0][1])
    for p, kind in enumerate(KIND):
        if kind == SHIFTED:
            a1(p)
    for step, p in ORDER[1:]:
        steps[step](p)
    g5(0)
    g5(1)
    flush()


def shards(tokens, gate_weight, up_weight, down_weight):
    depth, ff = gate_weight.shape
    quarters = tokens.reshape(4, 16, depth)
    wide = down_weight.shape[1]
    scratch = [
        pltpu.VMEM((depth, 2 * ff), BF16),
        pltpu.VMEM((ff, wide), BF16),
        pltpu.VMEM(tokens.shape, F32),
        pltpu.VMEM((2, 3, 32, wide), BF16),
    ]
    scratch += buffers(len(BIG), (2, 16), depth, ff, wide) + buffers(len(SMALL), (16,), depth, ff, wide)
    scratch += [
        pltpu.SemaphoreType.DMA((3, len(SENDS))),
        pltpu.SemaphoreType.DMA((len(RECEIVE),)),
        pltpu.SemaphoreType.DMA((4,)),
    ]
    whole = pl.BlockSpec(memory_space=pltpu.VMEM)
    anywhere = pl.BlockSpec(memory_space=pl.ANY)
    return pl.pallas_call(
        kernel,
        out_shape=jax.ShapeDtypeStruct(tokens.shape, BF16),
        in_specs=[anywhere] * 4,
        out_specs=whole,
        scratch_shapes=scratch,
        compiler_params=pltpu.CompilerParams(
            collective_id=0, has_side_effects=True, vmem_limit_bytes=60 << 20
        ),
        name="swiglu",
    )(quarters, gate_weight, up_weight, down_weight)


def solution(mesh):
    return jax.shard_map(
        shards,
        mesh=mesh,
        in_specs=(
            P(("gx", "gy"), "gz"),
            P("gz", ("gx", "gy")),
            P("gz", ("gx", "gy")),
            P(("gx", "gy"), "gz"),
        ),
        out_specs=P(("gx", "gy"), "gz"),
        check_vma=False,
    )
```

```python
import jax
import jax.numpy as jnp
from jax import lax
from jax.experimental import pallas as pl
from jax.experimental.pallas import tpu as pltpu
from jax.sharding import PartitionSpec as P

NEAR, FAR, HERE, SHIFTED = range(4)
PANELS = (
    (NEAR, 0, 0, 16), (NEAR, 0, 32, 16), (FAR, 0, 0, 16),
    (SHIFTED, 1, 0, 32), (SHIFTED, 3, 0, 32), (SHIFTED, 2, 0, 16),
    (SHIFTED, 2, 16, 16), (SHIFTED, 1, 32, 16), (SHIFTED, 1, 48, 16),
    (SHIFTED, 3, 32, 16), (SHIFTED, 3, 48, 16), (SHIFTED, 2, 32, 16),
    (SHIFTED, 2, 48, 16), (HERE, 0, 0, 16),
)
KIND = tuple(panel[0] for panel in PANELS)
OWN = KIND.index(HERE)
BIG = tuple(p for p, panel in enumerate(PANELS) if panel[3] == 32)
SMALL = tuple(p for p, panel in enumerate(PANELS) if panel[3] == 16 and p != OWN) + (OWN,)
BF16, F32 = jnp.bfloat16, jnp.float32
A2, A4, M1, X2, Z1, H, E1, E2, E3, M2, G2, G4 = range(12)
ORDER = (
    (A2, 0), (A2, 1), (A2, 2), (A2, 13), (A4, 13), (M1, 13), (A4, 0), (A4, 1),
    (M1, 0), (A2, 3), (A2, 5), (X2, 13), (A4, 2), (M1, 1), (M1, 2), (A2, 6),
    (A4, 3), (X2, 0), (A2, 10), (A2, 4), (A2, 12), (X2, 1), (M1, 3), (X2, 2),
    (A4, 5), (A4, 6), (Z1, 0), (Z1, 13), (A4, 10), (M1, 5), (A4, 4), (X2, 3),
    (Z1, 1), (M1, 4), (A4, 12), (Z1, 2), (A2, 11), (A2, 7), (A2, 9), (Z1, 3),
    (A2, 8), (X2, 5), (A4, 11), (M1, 10), (H, 13), (X2, 4), (Z1, 5), (H, 2),
    (A4, 9), (M1, 6), (M1, 11), (X2, 10), (H, 3), (M1, 12), (Z1, 4), (X2, 11),
    (E1, 2), (H, 5), (X2, 6), (E2, 2), (E1, 5), (M1, 9), (Z1, 10), (A4, 8),
    (H, 4), (X2, 12), (M1, 8), (A4, 7), (Z1, 6), (X2, 9), (Z1, 11), (M1, 7),
    (H, 10), (Z1, 12), (E2, 5), (E1, 3), (X2, 8), (E2, 3), (H, 6), (E3, 2),
    (H, 11), (X2, 7), (Z1, 9), (Z1, 8), (E1, 4), (E3, 3), (E2, 4), (H, 12),
    (M2, 2), (Z1, 7), (E3, 5), (E1, 10), (E2, 10), (E1, 11), (E2, 11), (M2, 3),
    (G2, 2), (E3, 4), (H, 9), (E1, 12), (M2, 5), (E2, 12), (H, 8), (H, 0),
    (E3, 10), (E3, 11), (E1, 6), (G2, 3), (H, 7), (E2, 6), (E1, 9), (M2, 4),
    (E2, 9), (E1, 8), (G2, 5), (H, 1), (E3, 12), (M2, 10), (E2, 8), (M2, 11),
    (E3, 6), (G2, 4), (E1, 7), (E3, 9), (G2, 10), (E2, 7), (E1, 0), (E2, 0),
    (M2, 12), (G2, 11), (E3, 8), (E1, 1), (G4, 3), (M2, 6), (E2, 1), (G4, 2),
    (M2, 9), (E3, 7), (G2, 12), (E3, 0), (G4, 4), (E1, 13), (G2, 6), (M2, 8),
    (G2, 9), (E2, 13), (E3, 1), (G4, 10), (M2, 7), (G4, 5), (G2, 8), (M2, 0),
    (G4, 12), (G4, 11), (G2, 7), (E3, 13), (M2, 1), (G2, 0), (G4, 6), (G4, 9),
    (G2, 1), (G4, 8), (G4, 7), (M2, 13), (G2, 13), (G4, 13), (G4, 0), (G4, 1),
)
FIRST_UP = next(p for step, p in ORDER if step == M1)
FIRST_DOWN = next(p for step, p in ORDER if step == M2)
ARRIVALS = ("az", "ay", "ac", "s1", "lo", "z", "ez", "e1", "e2", "gc", "gy")
SENDS = ("tokens", "sums", "hidden", "outputs")
RECEIVE = {
    key: i for i, key in enumerate(
        [(p, name) for p, kind in enumerate(KIND) for name in ARRIVALS
         if not (name == "az" and kind != SHIFTED or name in ("ay", "gy") and kind == HERE)]
        + [(0, "last"), (1, "last")]
    )
}
BUFFERS = (
    "tok", "part", "first", "second", "zsend", "zkeep", "zrecv", "hid", "outp", "crecv", "osum", "ysum", "zos"
)


def buffers(panels, tall, depth, ff, wide):
    rows = tall[0] * tall[-1] if len(tall) > 1 else tall[0]
    shapes = (
        (8,) + tall + (depth,), (8, rows, 2 * ff), (2, 2, rows, ff), (4, 2, rows, ff), (rows, 2 * ff),
        (rows, 2 * ff), (rows, 2 * ff), (8, rows, ff), (8, rows, wide), (4, rows, wide),
        (4, rows, wide), (4, rows, wide), (rows, wide),
    )
    return [
        pltpu.VMEM((panels,) + shape, F32 if name == "zkeep" else BF16)
        for name, shape in zip(BUFFERS, shapes)
    ]


def kernel(tokens, gate_hbm, up_hbm, down_hbm, out_hbm, out, wgu, wd, total, zor, *scratch):
    big = dict(zip(BUFFERS, scratch))
    small = dict(zip(BUFFERS, scratch[len(BUFFERS):]))
    send_sem, recv_sem, weight_sem = scratch[2 * len(BUFFERS):]
    gx, gy, gz = lax.axis_index("gx"), lax.axis_index("gy"), lax.axis_index("gz")
    x, h, y, c, zl = lax.rem(gz, 4), gz // 4, gx // 2, lax.rem(gx, 2), gy
    ff = gate_hbm.shape[1]

    def panel(p, name):
        group, members = (big, BIG) if p in BIG else (small, SMALL)
        return group[name].at[members.index(p)]

    def mod4(v):
        return lax.rem(v + 4, 4)

    def device(x=x, h=h, y=y, c=c, zl=zl):
        return {"gx": 2 * y + c, "gy": zl, "gz": 4 * h + x}

    xr, xl = device(x=mod4(x + 1)), device(x=mod4(x - 1))
    yr, yl, yf = device(y=mod4(y + 1)), device(y=mod4(y - 1)), device(y=mod4(y + 2))
    zpeer = device(h=1 - h)
    core = device(c=1 - c)
    zup = [None] + [device(zl=mod4(zl + k)) for k in (1, 2, 3)]
    zdown = [None, zup[3], zup[2], zup[1]]

    loads = [
        pltpu.make_async_copy(tokens, panel(OWN, "tok").at[pl.ds(4 * c, 4)], weight_sem.at[3]),
        pltpu.make_async_copy(gate_hbm, wgu.at[:, pl.ds(0, ff)], weight_sem.at[0]),
        pltpu.make_async_copy(up_hbm, wgu.at[:, pl.ds(ff, ff)], weight_sem.at[1]),
        pltpu.make_async_copy(down_hbm, wd, weight_sem.at[2]),
    ]
    barrier = pltpu.get_barrier_semaphore()
    peers = (xr, xl, yr, yl, yf, zpeer, core, zup[1], zup[2], zup[3])
    for peer in peers:
        pl.semaphore_signal(barrier, inc=1, device_id=peer, device_id_type=pl.DeviceIdType.MESH)
    for load in loads:
        load.start()
    cy = 4 * c + y
    total[...] = jnp.zeros_like(total)
    pl.semaphore_wait(barrier, len(peers))

    def arrival(p, name):
        return recv_sem.at[RECEIVE[p, name]]

    def send(p, group, name, src, dst, to):
        pltpu.make_async_remote_copy(
            src_ref=src, dst_ref=dst, send_sem=send_sem.at[2 if p == OWN else int(p in SMALL), SENDS.index(group)],
            recv_sem=arrival(PANELS[p][2] // 32 if name == "last" else p, name),
            device_id=to, device_id_type=pl.DeviceIdType.MESH,
        ).start()

    def arrived(p, name, extent):
        pltpu.make_async_remote_copy(
            src_ref=extent, dst_ref=extent, send_sem=send_sem.at[0, 0],
            recv_sem=arrival(p, name), device_id=core, device_id_type=pl.DeviceIdType.MESH,
        ).wait_recv()

    def flush():
        for i, name in enumerate(("tok", "part", "hid", "outp")):
            whole = name in ("tok", "outp")
            blocks, others = pl.ds(0, 8 if whole else 7), len(SMALL) - 1
            extents = (
                big[name].at[:, blocks], small[name].at[pl.ds(0, others), blocks],
                small[name].at[others, pl.ds(0, 4 if whole else 7)],
            )
            for k, extent in enumerate(extents):
                pltpu.make_async_remote_copy(
                    src_ref=extent, dst_ref=extent, send_sem=send_sem.at[k, i],
                    recv_sem=recv_sem.at[0], device_id=core, device_id_type=pl.DeviceIdType.MESH,
                ).wait_send()

    g, u = pl.ds(0, ff), pl.ds(ff, ff)

    def two(j):
        return pl.ds(2 * mod4(j), 2)

    def f32(v):
        return v.astype(F32)

    upper, lower = pl.ds(0, 2), pl.ds(2, 2)

    def a1(p):
        _, offset, row, rows = PANELS[p]
        source = tokens.at[pl.ds(row // 16, 2)] if rows == 32 else tokens.at[row // 16]
        send(p, "tokens", "az", source, panel(p, "tok").at[cy], zdown[offset])

    def a2(p):
        tok = panel(p, "tok")
        if KIND[p] == HERE:
            loads[0].wait()
        elif KIND[p] == NEAR:
            mine = tokens.at[pl.ds(PANELS[p][2] // 16, 2)]
            send(p, "tokens", "ay", mine, tok.at[pl.ds(4 * c + 2, 2)], yr)
            send(p, "tokens", "ay", mine, tok.at[pl.ds(4 * c, 2)], yl)
        elif KIND[p] == FAR:
            send(p, "tokens", "ay", tokens, tok.at[pl.ds(4 * c, 4)], yf)
        else:
            here = tok.at[cy]
            arrived(p, "az", here)
            send(p, "tokens", "ay", here, here, yf)
            send(p, "tokens", "ay", here, here, yr)
            send(p, "tokens", "ay", here, here, yl)

    def a4(p):
        tok = panel(p, "tok")
        if p != OWN:
            arrived(p, "ay", tok.at[pl.ds(0, 3 if KIND[p] == SHIFTED else 4)])
        here = tok.at[pl.ds(4 * c, 4)]
        send(p, "tokens", "ac", here, here, core)

    def m1(p):
        tok, part, first, second = (panel(p, n) for n in ("tok", "part", "first", "second"))
        arrived(p, "ac", tok.at[pl.ds(0, 4)])
        if p == FIRST_UP:
            loads[1].wait()
            loads[2].wait()
        rows = part.shape[1]

        def tile(i, carry):
            columns = pl.ds(pl.multiple_of(i * 256, 256), 256)
            lhs = tok[...].reshape(8 * rows, tok.shape[-1])
            product = jnp.dot(lhs, wgu[:, columns], preferred_element_type=F32)
            part[:, :, columns] = product.astype(BF16).reshape(8, rows, 256)
            return carry

        tiles = 2 * ff // 256
        lax.fori_loop(0, (tiles + 1) // 2, tile, 0)
        send(p, "sums", "s1", part.at[two(x + 2), :, g], first.at[0], xr)
        send(p, "sums", "lo", part.at[two(x - 1), :, g], second.at[1], xl)
        lax.fori_loop((tiles + 1) // 2, tiles, tile, 0)
        send(p, "sums", "s1", part.at[two(x + 2), :, u], first.at[1], xl)
        send(p, "sums", "lo", part.at[two(x + 1), :, u], second.at[3], xr)

    def x2(p):
        part, first, second = (panel(p, n) for n in ("part", "first", "second"))
        arrived(p, "s1", first)
        there = two(x + 1)
        part[there, :, g] = (f32(part[there, :, g]) + f32(first[0])).astype(BF16)
        send(p, "sums", "lo", part.at[there, :, g], second.at[0], xr)
        there = two(x - 1)
        part[there, :, u] = (f32(part[there, :, u]) + f32(first[1])).astype(BF16)
        send(p, "sums", "lo", part.at[there, :, u], second.at[2], xl)

    def z1(p):
        part, second = panel(p, "part"), panel(p, "second")
        zsend, zkeep, zrecv = (panel(p, n) for n in ("zsend", "zkeep", "zrecv"))
        arrived(p, "lo", second)

        def summed(b, cols, i):
            return f32(part[2 * x + b, :, cols]) + f32(second[i, b]) + f32(second[i + 1, b])

        zsend[:, g] = summed(1 - h, g, 0).astype(BF16)
        zsend[:, u] = summed(1 - h, u, 2).astype(BF16)
        send(p, "sums", "z", zsend, zrecv, zpeer)
        zkeep[:, g] = summed(h, g, 0)
        zkeep[:, u] = summed(h, u, 2)

    def hidden(p):
        hid, zkeep, zrecv = (panel(p, n) for n in ("hid", "zkeep", "zrecv"))
        arrived(p, "z", zrecv)
        gate = zkeep[:, g] + f32(zrecv[:, g])
        up = zkeep[:, u] + f32(zrecv[:, u])
        mine = 2 * x + h
        hid[mine] = (jax.nn.silu(gate) * up).astype(BF16)
        send(p, "hidden", "ez", hid.at[mine], hid.at[mine], zpeer)

    def e1(p):
        here = panel(p, "hid").at[2 * x + h]
        send(p, "hidden", "e1", here, here, xr)
        send(p, "hidden", "e2", here, here, xl)

    def e2(p):
        here = panel(p, "hid").at[2 * x + 1 - h]
        arrived(p, "ez", here)
        send(p, "hidden", "e1", here, here, xl)
        send(p, "hidden", "e2", here, here, xr)

    def e3(p):
        hid = panel(p, "hid")
        arrived(p, "e1", hid.at[pl.ds(0, 2)])
        here = hid.at[2 * mod4(x - 1) + h]
        send(p, "hidden", "e2", here, here, xr)
        here = hid.at[2 * mod4(x + 1) + 1 - h]
        send(p, "hidden", "e2", here, here, xl)

    def m2(p):
        hid, outp, crecv = (panel(p, n) for n in ("hid", "outp", "crecv"))
        arrived(p, "e2", hid.at[pl.ds(0, 4)])
        if p == FIRST_DOWN:
            loads[3].wait()
        rows = hid.shape[1]

        def tile(i, carry):
            columns = pl.ds(pl.multiple_of(i * 256, 256), 256)
            lhs = hid[...].reshape(8 * rows, ff)
            product = jnp.dot(lhs, wd[:, columns], preferred_element_type=F32)
            outp[:, :, columns] = product.astype(BF16).reshape(8, rows, 256)
            return carry

        lax.fori_loop(0, wd.shape[1] // 256, tile, 0)
        send(p, "outputs", "gc", outp.at[pl.ds(4 * (1 - c), 4)], crecv, core)

    def g2(p):
        outp, crecv, osum, ysum = (panel(p, n) for n in ("outp", "crecv", "osum", "ysum"))
        arrived(p, "gc", crecv)
        both = f32(outp[pl.ds(4 * c, 4)]) + f32(crecv[...])
        if p == OWN:
            total[...] += both.reshape(total.shape)
            return
        osum[...] = both.astype(BF16)
        if KIND[p] == NEAR:
            send(p, "outputs", "gy", osum.at[upper], ysum.at[upper], yr)
            send(p, "outputs", "gy", osum.at[lower], ysum.at[lower], yl)
        elif KIND[p] == FAR:
            send(p, "outputs", "gy", osum, ysum, yf)
        else:
            send(p, "outputs", "gy", osum.at[mod4(y + 2)], ysum.at[1], yf)
            send(p, "outputs", "gy", osum.at[mod4(y + 1)], ysum.at[0], yr)
            send(p, "outputs", "gy", osum.at[mod4(y - 1)], ysum.at[2], yl)

    def g4(p):
        osum, ysum, zos = (panel(p, n) for n in ("osum", "ysum", "zos"))
        if KIND[p] == NEAR:
            arrived(p, "gy", ysum)
            rows = pl.ds(PANELS[p][2], 32)
            total[rows] += (f32(ysum[upper]) + f32(ysum[lower])).reshape(32, total.shape[1])
        elif KIND[p] == FAR:
            arrived(p, "gy", ysum)
            total[...] += f32(ysum[...]).reshape(total.shape)
        elif KIND[p] == SHIFTED:
            _, offset, row, rows = PANELS[p]
            arrived(p, "gy", ysum.at[pl.ds(0, 3)])
            zos[...] = (f32(osum[y]) + f32(ysum[0]) + f32(ysum[1]) + f32(ysum[2])).astype(BF16)
            there = zor.at[row // 32, offset - 1, pl.ds(row % 32, rows)]
            send(p, "outputs", "last", zos, there, zup[offset])

    def g5(q):
        arrived(q, "last", zor.at[q])
        rows = pl.ds(32 * q, 32)
        whole = total[rows] + f32(zor[q, 0]) + f32(zor[q, 1]) + f32(zor[q, 2])
        out[rows, :] = whole.astype(BF16)
        pltpu.make_async_copy(out.at[rows], out_hbm.at[rows], weight_sem.at[4 + q]).start()

    steps = (a2, a4, m1, x2, z1, hidden, e1, e2, e3, m2, g2, g4)
    steps[ORDER[0][0]](ORDER[0][1])
    for p, kind in enumerate(KIND):
        if kind == SHIFTED:
            a1(p)
    for step, p in ORDER[1:]:
        steps[step](p)
    g5(0)
    g5(1)
    flush()
    for q in (0, 1):
        rows = pl.ds(32 * q, 32)
        pltpu.make_async_copy(out.at[rows], out_hbm.at[rows], weight_sem.at[4 + q]).wait()


def shards(tokens, gate_weight, up_weight, down_weight):
    depth, ff = gate_weight.shape
    quarters = tokens.reshape(4, 16, depth)
    wide = down_weight.shape[1]
    scratch = [
        pltpu.VMEM(tokens.shape, BF16),
        pltpu.VMEM((depth, 2 * ff), BF16),
        pltpu.VMEM((ff, wide), BF16),
        pltpu.VMEM(tokens.shape, F32),
        pltpu.VMEM((2, 3, 32, wide), BF16),
    ]
    scratch += buffers(len(BIG), (2, 16), depth, ff, wide) + buffers(len(SMALL), (16,), depth, ff, wide)
    scratch += [
        pltpu.SemaphoreType.DMA((3, len(SENDS))),
        pltpu.SemaphoreType.DMA((len(RECEIVE),)),
        pltpu.SemaphoreType.DMA((6,)),
    ]
    anywhere = pl.BlockSpec(memory_space=pl.ANY)
    return pl.pallas_call(
        kernel,
        out_shape=jax.ShapeDtypeStruct(tokens.shape, BF16),
        in_specs=[anywhere] * 4,
        out_specs=anywhere,
        scratch_shapes=scratch,
        compiler_params=pltpu.CompilerParams(
            collective_id=0, has_side_effects=True, vmem_limit_bytes=60 << 20
        ),
        name="swiglu",
    )(quarters, gate_weight, up_weight, down_weight)


def solution(mesh):
    return jax.shard_map(
        shards,
        mesh=mesh,
        in_specs=(
            P(("gx", "gy"), "gz"),
            P("gz", ("gx", "gy")),
            P("gz", ("gx", "gy")),
            P(("gx", "gy"), "gz"),
        ),
        out_specs=P(("gx", "gy"), "gz"),
        check_vma=False,
    )
```
